32 devices in a mesh: stream: 16 (over z, y, x), cross: 2 (over core).
Axes of the slice: x: 2, y: 2, z: 4, core: 2. Of those that a mesh axis runs over, the one named last changes fastest.
Arguments:
- vector: float32 [64, 4, 320], P('stream', 'cross'), may hold values from -2.5 to 2.5
- inverses: float32 [64, 4, 320, 320], P('stream', 'cross'), may hold values from -0.04 to 1
- lift_maps: float32 [4, 320, 80], replicated, may hold values from -1 to 1
- jacobians: float32 [64, 4, 4, 5, 5, 16], P('stream', 'cross'), may hold values from -0.2 to 1.43
- orient: int32 [64, 4], P('stream', 'cross'), may hold values from 0 to 7
Outputs:
- solution: float32 [64, 4, 320], P('stream', 'cross')
The draws below stay inside these ranges and needn't reach their ends.
All inputs are finite; a program needn't handle non-finite values.
Results may differ from the reference program's by a relative error of at most 0.0003.
Values sent between devices are 32-bit elements; how exact they have to be, the bound alone decides.
A program may use at most 64 MiB of HBM per device.

```python
import jax
import jax.numpy as jnp
from jax import lax

ORDER = 3
VARS = 5
NODES = 64
FACE = 16
BLOCK = 320
TRACE = 80
PASSES = 2
TOTAL_LAYERS = 64
TOTAL_CELLS = 4


def diagonal_draw(key):
    return jax.random.uniform(jax.random.fold_in(key, 11), (TOTAL_LAYERS, TOTAL_CELLS, BLOCK), jnp.float32, 0.7, 1.0)


def draw_inverses(key, part):
    full_shape = (TOTAL_LAYERS, TOTAL_CELLS, BLOCK, BLOCK)
    diagonal = diagonal_draw(key)
    key_off = jax.random.fold_in(key, 12)
    spread = jnp.clip(0.0095 * jax.random.normal(key_off, full_shape, jnp.float32), -0.04, 0.04)
    eye_mask = (jnp.arange(BLOCK)[:, None] == jnp.arange(BLOCK)[None, :]).astype(jnp.float32)
    return eye_mask * diagonal[..., None] + (1.0 - eye_mask) * spread


def draw_lift_maps(key, part):
    rows = jnp.arange(BLOCK, dtype=jnp.int32)
    var_of = rows // NODES
    remain = rows % NODES
    layer_of = remain // FACE
    node_of = remain % FACE
    trace_of = var_of * FACE + node_of
    columns = jnp.arange(TRACE, dtype=jnp.int32)
    match = (trace_of[:, None] == columns[None, :]).astype(jnp.float32)
    high_face = (layer_of == ORDER)[:, None]
    low_face = (layer_of == 0)[:, None]
    scale = 1.0 / jnp.sqrt(jnp.float32(TRACE))
    noise = jnp.clip(scale * jax.random.normal(key, (4, BLOCK, TRACE), jnp.float32), -4.0 * scale, 4.0 * scale)
    stream_low = jnp.where(high_face, -match, 0.35 * noise[0])
    stream_high = jnp.where(low_face, -match, 0.35 * noise[1])
    return jnp.stack([stream_low, stream_high, noise[2], noise[3]])


def draw_jacobians(key, part):
    extent = ORDER + 1
    full_shape = (TOTAL_LAYERS, TOTAL_CELLS, 4, VARS, VARS, FACE)
    rate_shape = (TOTAL_LAYERS, TOTAL_CELLS, 2, VARS, FACE)
    diagonal = diagonal_draw(key).reshape(TOTAL_LAYERS, TOTAL_CELLS, VARS, extent, FACE)
    face_diagonal = jnp.stack([diagonal[:, :, :, extent - 1], diagonal[:, :, :, 0]], axis=2)
    slow_share = 0.5
    sluggish_part = jax.random.bernoulli(jax.random.fold_in(key, 21), slow_share, (1, TOTAL_CELLS, 2, VARS, FACE))
    spread_power = jax.random.uniform(jax.random.fold_in(key, 22), (1, TOTAL_CELLS, 2, VARS, FACE), jnp.float32, 0.5, 1.5)
    gentle_decay_rate = jnp.exp(jnp.log(jnp.float32(0.25)) / TOTAL_LAYERS * spread_power)
    quick_decay_rate = jax.random.uniform(jax.random.fold_in(key, 23), rate_shape, jnp.float32, 0.85, 0.95)
    spike_factor = jax.random.bernoulli(jax.random.fold_in(key, 24), 2.0 / TOTAL_LAYERS, (TOTAL_LAYERS, TOTAL_CELLS, 2, 1, 1))
    residual_loss = jax.random.uniform(jax.random.fold_in(key, 25), rate_shape, jnp.float32, 0.6, 0.8)
    decay_rate = jnp.where(sluggish_part, gentle_decay_rate * jnp.where(spike_factor, residual_loss, 1.0), quick_decay_rate)
    stream_diagonal = decay_rate / face_diagonal
    cross_diagonal = jax.random.uniform(jax.random.fold_in(key, 26), rate_shape, jnp.float32, 0.5, 1.0)
    diagonal_all = jnp.concatenate([stream_diagonal, cross_diagonal], axis=2)
    face_scale = jnp.array([0.02, 0.02, 0.08, 0.08], jnp.float32)[None, None, :, None, None, None]
    key_off = jax.random.fold_in(key, 27)
    coupling = jnp.clip(face_scale * jax.random.normal(key_off, full_shape, jnp.float32), -2.5 * face_scale, 2.5 * face_scale)
    eye_mask = (jnp.arange(VARS)[:, None] == jnp.arange(VARS)[None, :]).astype(jnp.float32)[:, :, None]
    return eye_mask * diagonal_all[:, :, :, :, None, :] + (1.0 - eye_mask) * coupling


def touch_ends(entries, own_key, smallest, top_value):
    place = [jax.random.randint(jax.random.fold_in(own_key, axis), (), 0, length) for axis, length in enumerate(entries.shape)]
    longest = entries.shape.index(max(entries.shape))
    neighbour = place[:longest] + [(place[longest] + 1) % entries.shape[longest]] + place[longest + 1:]
    return entries.at[tuple(place)].set(smallest).at[tuple(neighbour)].set(top_value)


def shard_levels(own_key, shape, pieces, least, top_value):
    loudness = 1.0
    for position, blocks in pieces:
        steps = jax.random.uniform(jax.random.fold_in(jax.random.fold_in(own_key, 6), position), (blocks,), jnp.float32, least / len(pieces), top_value / len(pieces))
        loudness = loudness * jnp.repeat(jnp.exp(steps), shape[position] // blocks).reshape((-1,) + (1,) * (len(shape) - 1 - position))
    return loudness


def gaussian(own_key, shape, scale, bound, cuts=(), held_as=jnp.bfloat16):
    values = jax.random.normal(own_key, shape, jnp.float32) * scale
    if len(cuts) > 0:
        values = shard_levels(own_key, shape, cuts, -0.22, 0.18) * values
    return jnp.clip(values, min=-bound, max=bound).astype(held_as)


def setup_inputs(seed: int = 0) -> dict:
    arg_keys = jax.random.split(jax.random.key(seed), 6)
    return {
        "vector": gaussian(arg_keys[0], (TOTAL_LAYERS, TOTAL_CELLS, BLOCK), 0.25, 2.5, ((0, 16), (1, 2)), jnp.float32),
        "inverses": draw_inverses(jax.random.fold_in(arg_keys[5], 71), 0),
        "lift_maps": draw_lift_maps(jax.random.fold_in(arg_keys[5], 71), 0),
        "jacobians": draw_jacobians(jax.random.fold_in(arg_keys[5], 71), 0),
        "orient": touch_ends(jax.random.randint(arg_keys[4], (TOTAL_LAYERS, TOTAL_CELLS), 0, 8), jax.random.fold_in(arg_keys[4], 1), 0, 7).astype(jnp.int32),
    }


HIGHEST = lax.Precision.HIGHEST


def face_traces(field_values):
    extent = ORDER + 1
    node_cube = field_values.reshape(field_values.shape[:-1] + (VARS, extent, extent, extent))
    face_shape = field_values.shape[:-1] + (VARS, extent * extent)
    return (node_cube[..., 0, :, :].reshape(face_shape),
            node_cube[..., extent - 1, :, :].reshape(face_shape),
            node_cube[..., :, 0, :].reshape(face_shape),
            node_cube[..., :, extent - 1, :].reshape(face_shape))


def couple(lift_matrix, jacobian_face, face_trace):
    mixed_trace = jnp.einsum('...awf,...wf->...af', jacobian_face, face_trace, precision=HIGHEST)
    flat_trace = mixed_trace.reshape(mixed_trace.shape[:-2] + (TRACE,))
    return jnp.einsum('...t,rt->...r', flat_trace, lift_matrix, precision=HIGHEST)


def orient_tables():
    extent = ORDER + 1
    nodes_index = jnp.arange(extent * extent, dtype=jnp.int32)
    tables = []
    for variant in range(8):
        first_axis = nodes_index // extent
        second_axis = nodes_index % extent
        if variant % 2 == 1:
            first_axis, second_axis = second_axis, first_axis
        if (variant // 2) % 2 == 1:
            first_axis = extent - 1 - first_axis
        if (variant // 4) % 2 == 1:
            second_axis = extent - 1 - second_axis
        source_node = first_axis * extent + second_axis
        tables.append((source_node[:, None] == nodes_index[None, :]).astype(jnp.float32))
    return jnp.stack(tables)


def cross_load(field_values, lift_maps, jacobians, orient):
    chosen = (orient[..., None] == jnp.arange(8, dtype=jnp.int32)).astype(jnp.float32)
    picked = jnp.einsum('lco,odf->lcdf', chosen, orient_tables(), precision=HIGHEST)
    traces = face_traces(field_values)
    low_trace, high_trace = traces[2], traces[3]
    back_trace = jnp.einsum('lcdf,lcvd->lcvf', picked, low_trace, precision=HIGHEST)
    zero_rim = jnp.zeros_like(high_trace[:, :1])
    from_left = jnp.concatenate([zero_rim, high_trace[:, :-1]], axis=1)
    from_right = jnp.concatenate([back_trace[:, 1:], zero_rim], axis=1)
    mapped = jnp.einsum('lcdf,lcvf->lcvd', picked, from_left, precision=HIGHEST)
    return couple(lift_maps[2], jacobians[:, :, 2], mapped) + couple(lift_maps[3], jacobians[:, :, 3], from_right)


def line_sweep(right_side, inverses, lift_maps, jacobians):
    def forward(face_trace, layer_data):
        side_layer, inverse_layer, jacobian_layer = layer_data
        right_load = side_layer - couple(lift_maps[0], jacobian_layer[:, 0], face_trace)
        element_value = jnp.einsum('cij,cj->ci', inverse_layer, right_load, precision=HIGHEST)
        return face_traces(element_value)[1], element_value

    zero_trace = jnp.zeros((right_side.shape[1], VARS, FACE), jnp.float32)
    carried, lower_part = lax.scan(forward, zero_trace, (right_side, inverses, jacobians))

    def backward(face_trace, layer_data):
        lower_layer, inverse_layer, jacobian_layer = layer_data
        right_load = couple(lift_maps[1], jacobian_layer[:, 1], face_trace)
        element_value = lower_layer - jnp.einsum('cij,cj->ci', inverse_layer, right_load, precision=HIGHEST)
        return face_traces(element_value)[0], element_value

    carried, upper_part = lax.scan(backward, zero_trace, (lower_part, inverses, jacobians), reverse=True)
    return upper_part


def reference(vector, inverses, lift_maps, jacobians, orient):
    solution = line_sweep(vector, inverses, lift_maps, jacobians)
    for passage in range(PASSES - 1):
        solution = line_sweep(vector - cross_load(solution, lift_maps, jacobians, orient), inverses, lift_maps, jacobians)
    return solution
```

```python
import functools

import jax
import jax.numpy as jnp
import numpy as np
from jax import lax
from jax.experimental import pallas as pl
from jax.experimental.pallas import tpu as pltpu
from jax.sharding import PartitionSpec as P

ORDER = 3
EXTENT = ORDER + 1
VARS = 5
FACE = EXTENT * EXTENT
TRACE = VARS * FACE
BLOCK = VARS * FACE * EXTENT
SLOTS = (0, EXTENT - 1) + tuple(range(1, EXTENT - 1))
WIDE = 256
ROWS = TRACE + 8
F32 = jnp.float32
BF16 = jnp.bfloat16


def split(value):
    high = value.astype(BF16)
    return high, (value - high.astype(F32)).astype(BF16)


def product(left, right, transposed=False):
    dims = (((1,), (1 if transposed else 0,)), ((), ()))
    dot = functools.partial(lax.dot_general, dimension_numbers=dims, preferred_element_type=F32)
    left_high, left_low = left
    right_high, right_low = right
    return dot(left_high, right_high) + (dot(left_high, right_low) + dot(left_low, right_high))


def lanes(shape):
    return lax.broadcasted_iota(jnp.int32, shape, 1)


def rows(shape):
    return lax.broadcasted_iota(jnp.int32, shape, 0)


def keep(mask, value):
    return jnp.where(mask, value, 0.0)


def join(left, right):
    lane = lanes((TRACE, WIDE))
    through = jnp.concatenate(
        [jnp.zeros((TRACE, WIDE), F32), keep(lane < 2 * TRACE, right[:TRACE])], axis=0
    )
    first = product(split(left[:, : 2 * TRACE]), split(through))
    lane_all = lanes((ROWS, WIDE))
    row_all = rows((ROWS, WIDE))
    first = first + keep((lane_all >= 2 * TRACE) | (row_all >= TRACE), right)
    back = left[:TRACE]
    moved = pltpu.roll(back, WIDE - 2 * TRACE, 1)
    through = jnp.concatenate(
        [
            keep(lane < TRACE, moved),
            jnp.zeros((TRACE, WIDE), F32),
            keep(lane >= 2 * TRACE, back),
        ],
        axis=0,
    )
    second = product(split(first[:, : 3 * TRACE]), split(through))
    middle = (lane_all >= TRACE) & (lane_all < 2 * TRACE)
    return second + keep(middle, first) + keep(lane_all < TRACE, left)


def apply(column, matrix):
    return jnp.sum(column * matrix, axis=0, keepdims=True)


def stack(parts):
    total = jnp.zeros((8, parts[0].shape[1]), F32)
    row = rows(total.shape)
    for index, part in enumerate(parts):
        total = jnp.where(row == index, jnp.broadcast_to(part, total.shape), total)
    return total


def to_low(value):
    return keep(lanes(value.shape) < TRACE, pltpu.roll(value, WIDE - 2 * TRACE, 1))


def rise(z_left, z_right, left, right):
    lane = lanes((8, WIDE))
    column = z_left.T
    first = z_right + keep(
        lane < 2 * TRACE,
        stack([apply(column[TRACE : 2 * TRACE, c : c + 1], m) for c, m in enumerate(right)]),
    )
    column = first.T
    second = stack([apply(column[:TRACE, c : c + 1], m) for c, m in enumerate(left)])
    return to_low(second) + keep(lane < TRACE, z_left) + keep(lane >= TRACE, first)


def descend(z_in, z_left, z_right, left, right):
    lane = lanes((8, WIDE))
    high = (lane >= TRACE) & (lane < 2 * TRACE)
    column = z_in.T
    inner = keep(
        high,
        z_left + stack([apply(column[TRACE : 2 * TRACE, c : c + 1], m) for c, m in enumerate(left)]),
    )
    passed = stack([apply(column[:TRACE, c : c + 1], m) for c, m in enumerate(right)])
    column = inner.T
    turned = stack([apply(column[TRACE : 2 * TRACE, c : c + 1], m) for c, m in enumerate(right)])
    low = keep(lane < TRACE, z_right + turned) + to_low(passed)
    return low + keep(high, z_in), keep(lane < TRACE, z_in) + inner


def kernel(
    layers, cells, count, width, rounds,
    inv, lhs, faces, pick, out,
    blocks, block_sem, lhs_high, lhs_low, lifted, ends, sides, y, x,
    nodes, z_nodes, mine, theirs, send_sem, recv_sem, tail_sems,
    z_mine, z_theirs, z_send, z_recv,
    traces, backs, got_high, got_back, from_left, from_right, cross_sems,
):
    elements = layers * cells
    place = lax.axis_index("stream")
    column_at = lax.axis_index("cross")
    local = layers.bit_length() - 1

    copies = []
    for e in range(elements):
        for slot, i in enumerate(SLOTS):
            copy = pltpu.make_async_copy(inv.at[e, :, i], blocks.at[e, slot], block_sem.at[e, slot])
            copy.start()

    bits = [lax.rem(place // (1 << k), 2) for k in range(rounds)]
    partners = [place + (1 - 2 * bits[k]) * (1 << k) for k in range(rounds)]
    barrier = pltpu.get_barrier_semaphore()
    for k in range(rounds):
        pl.semaphore_signal(barrier, inc=1, device_id=(partners[k], column_at), device_id_type=pl.DeviceIdType.MESH)

    @pl.when(column_at > 0)
    def _():
        pl.semaphore_signal(barrier, inc=1, device_id=(place, column_at - 1), device_id_type=pl.DeviceIdType.MESH)

    @pl.when(column_at < width - 1)
    def _():
        pl.semaphore_signal(barrier, inc=1, device_id=(place, column_at + 1), device_id_type=pl.DeviceIdType.MESH)

    high, low = split(lhs[...])
    lhs_high[...] = high
    lhs_low[...] = low
    z_nodes[...] = jnp.zeros_like(z_nodes)
    z_mine[...] = jnp.zeros_like(z_mine)
    backs[...] = jnp.zeros_like(backs)

    lane = lanes((TRACE, WIDE))

    def prepare(e, carry):
        for slot, i in enumerate(SLOTS):
            pltpu.make_async_copy(inv.at[e, :, i], blocks.at[e, slot], block_sem.at[e, slot]).wait()
        block = split(blocks[e].reshape(BLOCK, BLOCK))
        through = product((lhs_high[...], lhs_low[...]), block, transposed=True)
        row_values = through[4 * TRACE : 4 * TRACE + elements]
        own = jnp.sum(keep(rows(row_values.shape) == e, row_values), axis=0, keepdims=True)
        y[pl.ds(e, 1), :] = own
        lifted[e] = through[2 * TRACE : 4 * TRACE]
        upward = -product(split(faces[e, 0]), split(through[:TRACE]))
        downward = -product(split(faces[e, 1]), split(through[TRACE : 2 * TRACE]))
        ends[e, :TRACE] = downward
        ends[e, TRACE:] = upward
        matrix = keep(lane < 2 * TRACE, upward[:, :WIDE]) + pltpu.roll(
            keep(lane < TRACE, downward[:, :WIDE]), 2 * TRACE, 1
        )
        nodes[e, :TRACE] = matrix
        bottom = keep(lanes((8, WIDE)) < 2 * TRACE, jnp.broadcast_to(own[:, :WIDE], (8, WIDE)))
        nodes[e, TRACE:] = keep(rows((8, WIDE)) == 0, bottom)
        return carry

    lax.fori_loop(0, elements, prepare, 0)

    starts = []
    base = 0
    for level in range(local + 1):
        starts.append(base)
        base += layers >> level

    def node(level, index, c):
        return (starts[level] + index) * cells + c

    for level in range(local):
        for index in range(layers >> (level + 1)):
            for c in range(cells):
                nodes[node(level + 1, index, c)] = join(
                    nodes[node(level, 2 * index, c)], nodes[node(level, 2 * index + 1, c)]
                )
    for c in range(cells):
        mine[0, c] = nodes[node(local, 0, c)]

    sides_met = jnp.minimum(column_at, 1) + jnp.minimum(width - 1 - column_at, 1)
    pl.semaphore_wait(barrier, rounds + sides_met)

    def remote(source, target, send, recv, device):
        return pltpu.make_async_remote_copy(
            src_ref=source, dst_ref=target, send_sem=send, recv_sem=recv,
            device_id=device, device_id_type=pl.DeviceIdType.MESH,
        )

    def prepare_sides(e, carry):
        for side in range(2):
            span = slice(side * TRACE, (side + 1) * TRACE)
            sides[e, span] = product(split(faces[e, 2 + side]), split(lifted[e, span]))
        return carry

    sent = []
    for k in range(rounds):
        device = (partners[k], column_at)
        if k < rounds - 1:
            pending = [remote(mine.at[k], theirs.at[k], send_sem.at[k], recv_sem.at[k], device)]
        else:
            pending = [
                remote(
                    mine.at[k, :, :, pl.ds(0, 128)], theirs.at[k, :, :, pl.ds(0, 128)],
                    send_sem.at[k], recv_sem.at[k], device,
                ),
                remote(
                    mine.at[k, :, pl.ds(TRACE, 8), pl.ds(128, 128)],
                    theirs.at[k, :, pl.ds(TRACE, 8), pl.ds(128, 128)],
                    tail_sems.at[0], tail_sems.at[1], device,
                ),
            ]
        for copy in pending:
            copy.start()
        sent += pending
        if k == 0:
            lax.fori_loop(0, elements, prepare_sides, 0)
        for copy in pending:
            copy.wait_recv()
        if k < rounds - 1:
            flag = bits[k] == 1
            for c in range(cells):
                ours, other = mine[k, c], theirs[k, c]
                mine[k + 1, c] = join(jnp.where(flag, other, ours), jnp.where(flag, ours, other))

    def ordered(k, c):
        flag = bits[k] == 1
        ours, other = mine[k, c, :TRACE], theirs[k, c, :TRACE]
        return jnp.where(flag, other, ours), jnp.where(flag, ours, other)

    def fall(z_pairs):
        lane_z = lanes((8, WIDE))
        z_in = None
        for k in reversed(range(rounds)):
            flag = bits[k] == 1
            ours, other = z_pairs[k]
            z_left, z_right = jnp.where(flag, other, ours), jnp.where(flag, ours, other)
            if z_in is None:
                column = z_left.T
                turned = stack([
                    apply(column[TRACE : 2 * TRACE, c : c + 1], theirs[k, c, :TRACE, :128])
                    for c in range(cells)
                ])
                turned = jnp.concatenate([turned, jnp.zeros((8, WIDE - 128), F32)], axis=1)
                z_low = keep(lane_z < TRACE, z_right + turned)
                z_high = keep((lane_z >= TRACE) & (lane_z < 2 * TRACE), z_left)
            else:
                pairs = [ordered(k, c) for c in range(cells)]
                z_low, z_high = descend(
                    z_in, z_left, z_right, [p[0] for p in pairs], [p[1] for p in pairs]
                )
            z_in = jnp.where(flag, z_high, z_low)
        entering = [z_in]
        for level in reversed(range(local)):
            following = []
            for index in range(layers >> (level + 1)):
                left = [nodes[node(level, 2 * index, c), :TRACE] for c in range(cells)]
                right = [nodes[node(level, 2 * index + 1, c), :TRACE] for c in range(cells)]
                following += list(
                    descend(
                        entering[index],
                        z_nodes[starts[level] + 2 * index],
                        z_nodes[starts[level] + 2 * index + 1],
                        left,
                        right,
                    )
                )
            entering = following
        for layer in range(layers):
            column = entering[layer].T
            for c in range(cells):
                e = layer * cells + c
                x[e : e + 1, :] = y[e : e + 1, :] + apply(column[: 2 * TRACE, c : c + 1], ends[e])

    for level in range(local):
        for index in range(layers >> level):
            for c in range(cells):
                z_nodes[starts[level] + index, c : c + 1, :] = nodes[node(level, index, c), TRACE : TRACE + 1]
    fall([
        (
            stack([mine[k, c, TRACE : TRACE + 1] for c in range(cells)]),
            stack([theirs[k, c, TRACE : TRACE + 1] for c in range(cells)]),
        )
        for k in range(rounds)
    ])

    x_high, x_low = split(x[...])
    cross = jnp.dot(x_high, pick[...], preferred_element_type=F32) + jnp.dot(
        x_low, pick[...], preferred_element_type=F32
    )
    traces[...] = cross[:, 128:]
    column = cross[:, :128].T
    for e in range(elements):
        backs[e : e + 1, :TRACE] = apply(column[:TRACE, e : e + 1], faces[e, 4])
    up = remote(traces, got_high, cross_sems.at[0], cross_sems.at[1], (place, lax.rem(column_at + 1, width)))
    down = remote(backs, got_back, cross_sems.at[2], cross_sems.at[3], (place, lax.rem(column_at + width - 1, width)))

    @pl.when(column_at < width - 1)
    def _():
        up.start()

    @pl.when(column_at > 0)
    def _():
        down.start()

    for layer in range(layers):
        for c in range(cells):
            e = layer * cells + c
            if c > 0:
                from_left[e : e + 1, :] = traces[e - 1 : e, :]
            if c < cells - 1:
                from_right[e : e + 1, :] = backs[e + 1 : e + 2, :]
    firsts = [layer * cells for layer in range(layers)]
    lasts = [layer * cells + cells - 1 for layer in range(layers)]

    @pl.when(column_at > 0)
    def _():
        up.wait_recv()
        for first, last in zip(firsts, lasts):
            from_left[first : first + 1, :] = got_high[last : last + 1, :]

    @pl.when(column_at == 0)
    def _():
        for first in firsts:
            from_left[first : first + 1, :] = jnp.zeros((1, 128), F32)

    @pl.when(column_at < width - 1)
    def _():
        down.wait_recv()
        for first, last in zip(firsts, lasts):
            from_right[last : last + 1, :] = got_back[first : first + 1, :]

    @pl.when(column_at == width - 1)
    def _():
        for last in lasts:
            from_right[last : last + 1, :] = jnp.zeros((1, 128), F32)

    left_columns = from_left[...].T
    right_columns = from_right[...].T
    lane_row = lanes((1, WIDE))
    for layer in range(layers):
        for c in range(cells):
            e = layer * cells + c
            value = y[e : e + 1, :] - (
                apply(left_columns[:TRACE, e : e + 1], sides[e, :TRACE])
                + apply(right_columns[:TRACE, e : e + 1], sides[e, TRACE:])
            )
            y[e : e + 1, :] = value
            z_nodes[starts[0] + layer, c : c + 1, :] = keep(lane_row < 2 * TRACE, value[:, :WIDE])

    for level in range(local):
        for index in range(layers >> (level + 1)):
            left = [nodes[node(level, 2 * index, c), :TRACE] for c in range(cells)]
            right = [nodes[node(level, 2 * index + 1, c), :TRACE] for c in range(cells)]
            z_nodes[starts[level + 1] + index] = rise(
                z_nodes[starts[level] + 2 * index], z_nodes[starts[level] + 2 * index + 1], left, right
            )
    z_mine[0] = z_nodes[starts[local]]
    for k in range(rounds):
        copy = remote(z_mine.at[k], z_theirs.at[k], z_send.at[k], z_recv.at[k], (partners[k], column_at))
        copy.start()
        sent.append(copy)
        if k < rounds - 1:
            pairs = [ordered(k, c) for c in range(cells)]
        copy.wait_recv()
        if k < rounds - 1:
            flag = bits[k] == 1
            ours, other = z_mine[k], z_theirs[k]
            z_mine[k + 1] = rise(
                jnp.where(flag, other, ours), jnp.where(flag, ours, other),
                [p[0] for p in pairs], [p[1] for p in pairs],
            )
    fall([(z_mine[k], z_theirs[k]) for k in range(rounds)])
    out[...] = x[...]

    for copy in sent:
        copy.wait_send()

    @pl.when(column_at < width - 1)
    def _():
        up.wait_send()

    @pl.when(column_at > 0)
    def _():
        down.wait_send()


def picker():
    table = np.zeros((BLOCK, WIDE), np.float32)
    for slot, i in enumerate(SLOTS):
        for v in range(VARS):
            for k in range(EXTENT):
                source = slot * TRACE + v * FACE + k
                target = v * FACE + i * EXTENT + k
                table[source, target] = 1.0
                table[source + (EXTENT - 1) * EXTENT, 128 + target] = 1.0
    return table


def face_sources():
    nodes_index = np.arange(FACE)
    sources = []
    for variant in range(8):
        first, second = nodes_index // EXTENT, nodes_index % EXTENT
        if variant % 2 == 1:
            first, second = second, first
        if variant // 2 % 2 == 1:
            first = EXTENT - 1 - first
        if variant // 4 % 2 == 1:
            second = EXTENT - 1 - second
        sources.append(first * EXTENT + second)
    source = np.stack(sources)
    return (source[:, :, None] == nodes_index).astype(np.float32)


def on_device(width, count, vector, inverses, lift_maps, jacobians, orient):
    layers, cells = vector.shape[:2]
    elements = layers * cells
    rounds = count.bit_length() - 1
    inv = inverses.reshape(elements, VARS, EXTENT, FACE, BLOCK)
    lift_rows = lift_maps.transpose(0, 2, 1).reshape(4 * TRACE, BLOCK)
    lhs = jnp.concatenate(
        [lift_rows, vector.reshape(elements, BLOCK), jnp.zeros((-elements % 16, BLOCK), F32)], axis=0
    )
    chosen = (orient.reshape(elements, 1) == jnp.arange(8, dtype=jnp.int32)).astype(F32)
    oriented = jnp.sum(chosen[:, :, None, None] * jnp.asarray(face_sources()), axis=1)
    same = jnp.broadcast_to(jnp.eye(FACE, dtype=F32), (elements, FACE, FACE))
    source_maps = jnp.stack([same, same, oriented, same], axis=1)
    turned = jacobians.reshape(elements, 4, VARS, VARS, FACE).transpose(0, 1, 3, 2, 4)
    faces = (
        turned[:, :, :, None, :, :] * source_maps.transpose(0, 1, 3, 2)[:, :, None, :, None, :]
    ).reshape(elements, 4, TRACE, TRACE)
    back = (jnp.eye(VARS, dtype=F32)[:, None, :, None] * oriented[:, None, :, None, :]).reshape(
        elements, 1, TRACE, TRACE
    )
    faces = jnp.concatenate([faces, back], axis=1)
    pick = jnp.asarray(picker(), BF16)
    total_nodes = 2 * layers - 1
    vmem = pl.BlockSpec(memory_space=pltpu.VMEM)
    result = pl.pallas_call(
        functools.partial(kernel, layers, cells, count, width, rounds),
        out_shape=jax.ShapeDtypeStruct((elements, BLOCK), F32),
        in_specs=[pl.BlockSpec(memory_space=pl.ANY), vmem, vmem, vmem],
        out_specs=vmem,
        scratch_shapes=[
            pltpu.VMEM((elements, EXTENT, VARS, FACE, BLOCK), F32),
            pltpu.SemaphoreType.DMA((elements, EXTENT)),
            pltpu.VMEM(lhs.shape, BF16),
            pltpu.VMEM(lhs.shape, BF16),
            pltpu.VMEM((elements, 2 * TRACE, BLOCK), F32),
            pltpu.VMEM((elements, 2 * TRACE, BLOCK), F32),
            pltpu.VMEM((elements, 2 * TRACE, BLOCK), F32),
            pltpu.VMEM((elements, BLOCK), F32),
            pltpu.VMEM((elements, BLOCK), F32),
            pltpu.VMEM((total_nodes * cells, ROWS, WIDE), F32),
            pltpu.VMEM((total_nodes, 8, WIDE), F32),
            pltpu.VMEM((rounds, cells, ROWS, WIDE), F32),
            pltpu.VMEM((rounds, cells, ROWS, WIDE), F32),
            pltpu.SemaphoreType.DMA((rounds,)),
            pltpu.SemaphoreType.DMA((rounds,)),
            pltpu.SemaphoreType.DMA((2,)),
            pltpu.VMEM((rounds, 8, WIDE), F32),
            pltpu.VMEM((rounds, 8, WIDE), F32),
            pltpu.SemaphoreType.DMA((rounds,)),
            pltpu.SemaphoreType.DMA((rounds,)),
            pltpu.VMEM((elements, 128), F32),
            pltpu.VMEM((elements, 128), F32),
            pltpu.VMEM((elements, 128), F32),
            pltpu.VMEM((elements, 128), F32),
            pltpu.VMEM((elements, 128), F32),
            pltpu.VMEM((elements, 128), F32),
            pltpu.SemaphoreType.DMA((4,)),
        ],
        compiler_params=pltpu.CompilerParams(
            collective_id=0, has_side_effects=True, vmem_limit_bytes=48 * 1024 * 1024
        ),
    )(inv, lhs, faces, pick)
    cube = result.reshape(elements, EXTENT, VARS, FACE)
    order = [SLOTS.index(i) for i in range(EXTENT)]
    natural = jnp.stack([cube[:, slot] for slot in order], axis=2)
    return natural.reshape(layers, cells, BLOCK)


def solution(mesh):
    in_specs = (
        P("stream", "cross", None),
        P("stream", "cross", None, None),
        P(),
        P("stream", "cross", None, None, None, None),
        P("stream", "cross"),
    )
    out_specs = P("stream", "cross", None)
    return jax.shard_map(
        functools.partial(on_device, mesh.shape["cross"], mesh.shape["stream"]),
        mesh=mesh, in_specs=in_specs, out_specs=out_specs, check_vma=False,
    )
```

```python
import functools

import jax
import jax.numpy as jnp
import numpy as np
from jax import lax
from jax.experimental import pallas as pl
from jax.experimental.pallas import tpu as pltpu
from jax.sharding import PartitionSpec as P

ORDER = 3
EXTENT = ORDER + 1
VARS = 5
FACE = EXTENT * EXTENT
TRACE = VARS * FACE
BLOCK = VARS * FACE * EXTENT
SLOTS = (0, EXTENT - 1) + tuple(range(1, EXTENT - 1))
WIDE = 256
ROWS = TRACE + 8
F32 = jnp.float32
BF16 = jnp.bfloat16


def split(value):
    high = value.astype(BF16)
    return high, (value - high.astype(F32)).astype(BF16)


def product(left, right, transposed=False):
    dims = (((1,), (1 if transposed else 0,)), ((), ()))
    dot = functools.partial(lax.dot_general, dimension_numbers=dims, preferred_element_type=F32)
    left_high, left_low = left
    right_high, right_low = right
    return dot(left_high, right_high) + (dot(left_high, right_low) + dot(left_low, right_high))


def lanes(shape):
    return lax.broadcasted_iota(jnp.int32, shape, 1)


def rows(shape):
    return lax.broadcasted_iota(jnp.int32, shape, 0)


def keep(mask, value):
    return jnp.where(mask, value, 0.0)


def join(left, right):
    lane = lanes((TRACE, WIDE))
    through = jnp.concatenate(
        [jnp.zeros((TRACE, WIDE), F32), keep(lane < 2 * TRACE, right[:TRACE])], axis=0
    )
    first = product(split(left[:, : 2 * TRACE]), split(through))
    lane_all = lanes((ROWS, WIDE))
    row_all = rows((ROWS, WIDE))
    first = first + keep((lane_all >= 2 * TRACE) | (row_all >= TRACE), right)
    back = left[:TRACE]
    moved = pltpu.roll(back, WIDE - 2 * TRACE, 1)
    through = jnp.concatenate(
        [
            keep(lane < TRACE, moved),
            jnp.zeros((TRACE, WIDE), F32),
            keep(lane >= 2 * TRACE, back),
        ],
        axis=0,
    )
    second = product(split(first[:, : 3 * TRACE]), split(through))
    middle = (lane_all >= TRACE) & (lane_all < 2 * TRACE)
    return second + keep(middle, first) + keep(lane_all < TRACE, left)


def apply(column, matrix):
    return jnp.sum(column * matrix, axis=0, keepdims=True)


def stack(parts):
    total = jnp.zeros((8, parts[0].shape[1]), F32)
    row = rows(total.shape)
    for index, part in enumerate(parts):
        total = jnp.where(row == index, jnp.broadcast_to(part, total.shape), total)
    return total


def to_low(value):
    return keep(lanes(value.shape) < TRACE, pltpu.roll(value, WIDE - 2 * TRACE, 1))


def rise(z_left, z_right, left, right):
    lane = lanes((8, WIDE))
    column = z_left.T
    first = z_right + keep(
        lane < 2 * TRACE,
        stack([apply(column[TRACE : 2 * TRACE, c : c + 1], m) for c, m in enumerate(right)]),
    )
    column = first.T
    second = stack([apply(column[:TRACE, c : c + 1], m) for c, m in enumerate(left)])
    return to_low(second) + keep(lane < TRACE, z_left) + keep(lane >= TRACE, first)


def descend(z_in, z_left, z_right, left, right):
    lane = lanes((8, WIDE))
    high = (lane >= TRACE) & (lane < 2 * TRACE)
    column = z_in.T
    inner = keep(
        high,
        z_left + stack([apply(column[TRACE : 2 * TRACE, c : c + 1], m) for c, m in enumerate(left)]),
    )
    passed = stack([apply(column[:TRACE, c : c + 1], m) for c, m in enumerate(right)])
    column = inner.T
    turned = stack([apply(column[TRACE : 2 * TRACE, c : c + 1], m) for c, m in enumerate(right)])
    low = keep(lane < TRACE, z_right + turned) + to_low(passed)
    return low + keep(high, z_in), keep(lane < TRACE, z_in) + inner


def kernel(
    layers, cells, count, width, rounds,
    inv, vector, lift_maps, jacobians, orient, pick, out,
    blocks, block_sem, lhs, jac_rows, natural, lhs_high, lhs_low, lifted, ends, sides, y, x,
    nodes, z_nodes, mine, theirs, send_sem, recv_sem, tail_sems,
    z_mine, z_theirs, z_send, z_recv,
    traces, backs, got_high, got_back, from_left, from_right, cross_sems,
):
    elements = layers * cells
    place = lax.axis_index("stream")
    column_at = lax.axis_index("cross")
    local = layers.bit_length() - 1

    copies = []
    for e in range(elements):
        for slot, i in enumerate(SLOTS):
            copy = pltpu.make_async_copy(inv.at[e, :, i], blocks.at[e, slot], block_sem.at[e, slot])
            copy.start()

    bits = [lax.rem(place // (1 << k), 2) for k in range(rounds)]
    partners = [place + (1 - 2 * bits[k]) * (1 << k) for k in range(rounds)]
    barrier = pltpu.get_barrier_semaphore()
    for k in range(rounds):
        pl.semaphore_signal(barrier, inc=1, device_id=(partners[k], column_at), device_id_type=pl.DeviceIdType.MESH)

    @pl.when(column_at > 0)
    def _():
        pl.semaphore_signal(barrier, inc=1, device_id=(place, column_at - 1), device_id_type=pl.DeviceIdType.MESH)

    @pl.when(column_at < width - 1)
    def _():
        pl.semaphore_signal(barrier, inc=1, device_id=(place, column_at + 1), device_id_type=pl.DeviceIdType.MESH)

    for m in range(4):
        lhs[m * TRACE : (m + 1) * TRACE, :] = lift_maps[m]
    lhs[4 * TRACE :, :] = jnp.zeros((lhs.shape[0] - 4 * TRACE, BLOCK), F32)
    for e in range(elements):
        lhs[4 * TRACE + e : 4 * TRACE + e + 1, :] = vector[e // cells, e % cells : e % cells + 1, :]
        for v in range(VARS):
            for w in range(VARS):
                jac_rows[e, w, :4, v * FACE : (v + 1) * FACE] = jacobians[e, v, w]
    high, low = split(lhs[...])
    lhs_high[...] = high
    lhs_low[...] = low
    z_nodes[...] = jnp.zeros_like(z_nodes)
    z_mine[...] = jnp.zeros_like(z_mine)
    backs[...] = jnp.zeros_like(backs)

    lane = lanes((TRACE, WIDE))

    row_face = rows((TRACE, TRACE))
    lane_face = lanes((TRACE, TRACE))
    same = lax.rem(row_face, FACE) == lax.rem(lane_face, FACE)

    def source_of(code, node_index):
        first, second = node_index // EXTENT, lax.rem(node_index, EXTENT)
        first, second = (
            first + lax.rem(code, 2) * (second - first),
            second + lax.rem(code, 2) * (first - second),
        )
        first = first + lax.rem(code // 2, 2) * (EXTENT - 1 - 2 * first)
        second = second + lax.rem(code // 4, 2) * (EXTENT - 1 - 2 * second)
        return first * EXTENT + second

    def face(e, m, chosen):
        tall = jnp.concatenate(
            [jnp.broadcast_to(jac_rows[e, w, m : m + 1, :TRACE], (FACE, TRACE)) for w in range(VARS)],
            axis=0,
        )
        return keep(chosen, tall)

    def prepare_layer(layer, carry):
        for c in range(cells):
            prepare(layer * cells + c)
        return carry

    def prepare(e):
        for slot, i in enumerate(SLOTS):
            pltpu.make_async_copy(inv.at[e, :, i], blocks.at[e, slot], block_sem.at[e, slot]).wait()
        block = split(blocks[e].reshape(BLOCK, BLOCK))
        through = product((lhs_high[...], lhs_low[...]), block, transposed=True)
        row_values = through[4 * TRACE : 4 * TRACE + elements]
        own = jnp.sum(keep(rows(row_values.shape) == e, row_values), axis=0, keepdims=True)
        y[pl.ds(e, 1), :] = own
        lifted[e] = through[2 * TRACE : 4 * TRACE]
        upward = -product(split(face(e, 0, same)), split(through[:TRACE]))
        downward = -product(split(face(e, 1, same)), split(through[TRACE : 2 * TRACE]))
        ends[e, :TRACE] = downward
        ends[e, TRACE:] = upward
        matrix = keep(lane < 2 * TRACE, upward[:, :WIDE]) + pltpu.roll(
            keep(lane < TRACE, downward[:, :WIDE]), 2 * TRACE, 1
        )
        nodes[e, :TRACE] = matrix
        bottom = keep(lanes((8, WIDE)) < 2 * TRACE, jnp.broadcast_to(own[:, :WIDE], (8, WIDE)))
        nodes[e, TRACE:] = keep(rows((8, WIDE)) == 0, bottom)

    lax.fori_loop(0, layers, prepare_layer, 0)

    sides_met = jnp.minimum(column_at, 1) + jnp.minimum(width - 1 - column_at, 1)
    pl.semaphore_wait(barrier, rounds + sides_met)

    starts = []
    base = 0
    for level in range(local + 1):
        starts.append(base)
        base += layers >> level

    def node(level, index, c):
        return (starts[level] + index) * cells + c

    def remote(source, target, send, recv, device):
        return pltpu.make_async_remote_copy(
            src_ref=source, dst_ref=target, send_sem=send, recv_sem=recv,
            device_id=device, device_id_type=pl.DeviceIdType.MESH,
        )

    sent = []
    pending = {}

    def dispatch(k, c):
        device = (partners[k], column_at)
        send, recv = send_sem.at[k, c], recv_sem.at[k, c]
        if k < rounds - 1:
            pending[k, c] = [remote(mine.at[k, c], theirs.at[k, c], send, recv, device)]
        else:
            first, second = pl.ds(0, 128), pl.ds(128, 128)
            bottom = pl.ds(TRACE, 8)
            pending[k, c] = [
                remote(mine.at[k, c, :, first], theirs.at[k, c, :, first], send, recv, device),
                remote(
                    mine.at[k, c, bottom, second], theirs.at[k, c, bottom, second],
                    tail_sems.at[0, c], tail_sems.at[1, c], device,
                ),
            ]
        for copy in pending[k, c]:
            copy.start()
            sent.append(copy)

    for c in range(cells):
        for level in range(local):
            for index in range(layers >> (level + 1)):
                nodes[node(level + 1, index, c)] = join(
                    nodes[node(level, 2 * index, c)], nodes[node(level, 2 * index + 1, c)]
                )
        mine[0, c] = nodes[node(local, 0, c)]
        dispatch(0, c)

    def prepare_sides(layer, carry):
        for c in range(cells):
            e = layer * cells + c
            chosen = lax.rem(row_face, FACE) == source_of(orient[c, layer], lax.rem(lane_face, FACE))
            sides[e, :TRACE] = product(split(face(e, 2, chosen)), split(lifted[e, :TRACE]))
            sides[e, TRACE:] = product(split(face(e, 3, same)), split(lifted[e, TRACE:]))
        return carry

    lax.fori_loop(0, layers, prepare_sides, 0)

    for k in range(rounds):
        for c in range(cells):
            for copy in pending[k, c]:
                copy.wait_recv()
            if k < rounds - 1:
                flag = bits[k] == 1
                ours, other = mine[k, c], theirs[k, c]
                mine[k + 1, c] = join(jnp.where(flag, other, ours), jnp.where(flag, ours, other))
                dispatch(k + 1, c)

    def ordered(k, c):
        flag = bits[k] == 1
        ours, other = mine[k, c, :TRACE], theirs[k, c, :TRACE]
        return jnp.where(flag, other, ours), jnp.where(flag, ours, other)

    def fall(z_pairs):
        lane_z = lanes((8, WIDE))
        z_in = None
        for k in reversed(range(rounds)):
            flag = bits[k] == 1
            ours, other = z_pairs[k]
            z_left, z_right = jnp.where(flag, other, ours), jnp.where(flag, ours, other)
            if z_in is None:
                column = z_left.T
                turned = stack([
                    apply(column[TRACE : 2 * TRACE, c : c + 1], theirs[k, c, :TRACE, :128])
                    for c in range(cells)
                ])
                turned = jnp.concatenate([turned, jnp.zeros((8, WIDE - 128), F32)], axis=1)
                z_low = keep(lane_z < TRACE, z_right + turned)
                z_high = keep((lane_z >= TRACE) & (lane_z < 2 * TRACE), z_left)
            else:
                pairs = [ordered(k, c) for c in range(cells)]
                z_low, z_high = descend(
                    z_in, z_left, z_right, [p[0] for p in pairs], [p[1] for p in pairs]
                )
            z_in = jnp.where(flag, z_high, z_low)
        entering = [z_in]
        for level in reversed(range(local)):
            following = []
            for index in range(layers >> (level + 1)):
                left = [nodes[node(level, 2 * index, c), :TRACE] for c in range(cells)]
                right = [nodes[node(level, 2 * index + 1, c), :TRACE] for c in range(cells)]
                following += list(
                    descend(
                        entering[index],
                        z_nodes[starts[level] + 2 * index],
                        z_nodes[starts[level] + 2 * index + 1],
                        left,
                        right,
                    )
                )
            entering = following
        for layer in range(layers):
            column = entering[layer].T
            for c in range(cells):
                e = layer * cells + c
                x[e : e + 1, :] = y[e : e + 1, :] + apply(column[: 2 * TRACE, c : c + 1], ends[e])

    for level in range(local):
        for index in range(layers >> level):
            for c in range(cells):
                z_nodes[starts[level] + index, c : c + 1, :] = nodes[node(level, index, c), TRACE : TRACE + 1]
    fall([
        (
            stack([mine[k, c, TRACE : TRACE + 1] for c in range(cells)]),
            stack([theirs[k, c, TRACE : TRACE + 1] for c in range(cells)]),
        )
        for k in range(rounds)
    ])

    x_high, x_low = split(x[...])
    cross = jnp.dot(x_high, pick[...], preferred_element_type=F32) + jnp.dot(
        x_low, pick[...], preferred_element_type=F32
    )
    traces[...] = cross[:, 128:]
    column = cross[:, :128].T
    for e in range(elements):
        turn = (row_face // FACE == lane_face // FACE) & (
            source_of(orient[e % cells, e // cells], lax.rem(row_face, FACE)) == lax.rem(lane_face, FACE)
        )
        backs[e : e + 1, :TRACE] = apply(column[:TRACE, e : e + 1], turn.astype(F32))
    up = remote(traces, got_high, cross_sems.at[0], cross_sems.at[1], (place, lax.rem(column_at + 1, width)))
    down = remote(backs, got_back, cross_sems.at[2], cross_sems.at[3], (place, lax.rem(column_at + width - 1, width)))

    @pl.when(column_at < width - 1)
    def _():
        up.start()

    @pl.when(column_at > 0)
    def _():
        down.start()

    for layer in range(layers):
        for c in range(cells):
            e = layer * cells + c
            if c > 0:
                from_left[e : e + 1, :] = traces[e - 1 : e, :]
            if c < cells - 1:
                from_right[e : e + 1, :] = backs[e + 1 : e + 2, :]
    firsts = [layer * cells for layer in range(layers)]
    lasts = [layer * cells + cells - 1 for layer in range(layers)]

    @pl.when(column_at > 0)
    def _():
        up.wait_recv()
        for first, last in zip(firsts, lasts):
            from_left[first : first + 1, :] = got_high[last : last + 1, :]

    @pl.when(column_at == 0)
    def _():
        for first in firsts:
            from_left[first : first + 1, :] = jnp.zeros((1, 128), F32)

    @pl.when(column_at < width - 1)
    def _():
        down.wait_recv()
        for first, last in zip(firsts, lasts):
            from_right[last : last + 1, :] = got_back[first : first + 1, :]

    @pl.when(column_at == width - 1)
    def _():
        for last in lasts:
            from_right[last : last + 1, :] = jnp.zeros((1, 128), F32)

    left_columns = from_left[...].T
    right_columns = from_right[...].T
    lane_row = lanes((1, WIDE))
    for layer in range(layers):
        for c in range(cells):
            e = layer * cells + c
            value = y[e : e + 1, :] - (
                apply(left_columns[:TRACE, e : e + 1], sides[e, :TRACE])
                + apply(right_columns[:TRACE, e : e + 1], sides[e, TRACE:])
            )
            y[e : e + 1, :] = value
            z_nodes[starts[0] + layer, c : c + 1, :] = keep(lane_row < 2 * TRACE, value[:, :WIDE])

    for level in range(local):
        for index in range(layers >> (level + 1)):
            left = [nodes[node(level, 2 * index, c), :TRACE] for c in range(cells)]
            right = [nodes[node(level, 2 * index + 1, c), :TRACE] for c in range(cells)]
            z_nodes[starts[level + 1] + index] = rise(
                z_nodes[starts[level] + 2 * index], z_nodes[starts[level] + 2 * index + 1], left, right
            )
    z_mine[0] = z_nodes[starts[local]]
    for k in range(rounds):
        copy = remote(z_mine.at[k], z_theirs.at[k], z_send.at[k], z_recv.at[k], (partners[k], column_at))
        copy.start()
        sent.append(copy)
        if k < rounds - 1:
            pairs = [ordered(k, c) for c in range(cells)]
        copy.wait_recv()
        if k < rounds - 1:
            flag = bits[k] == 1
            ours, other = z_mine[k], z_theirs[k]
            z_mine[k + 1] = rise(
                jnp.where(flag, other, ours), jnp.where(flag, ours, other),
                [p[0] for p in pairs], [p[1] for p in pairs],
            )
    fall([(z_mine[k], z_theirs[k]) for k in range(rounds)])
    for slot, i in enumerate(SLOTS):
        for v in range(VARS):
            target = (v * EXTENT + i) * FACE
            source = slot * TRACE + v * FACE
            natural[:, target : target + FACE] = x[:, source : source + FACE]
    for layer in range(layers):
        out[layer] = natural[layer * cells : (layer + 1) * cells, :]

    for copy in sent:
        copy.wait_send()

    @pl.when(column_at < width - 1)
    def _():
        up.wait_send()

    @pl.when(column_at > 0)
    def _():
        down.wait_send()


def picker():
    table = np.zeros((BLOCK, WIDE), np.float32)
    for slot, i in enumerate(SLOTS):
        for v in range(VARS):
            for k in range(EXTENT):
                source = slot * TRACE + v * FACE + k
                target = v * FACE + i * EXTENT + k
                table[source, target] = 1.0
                table[source + (EXTENT - 1) * EXTENT, 128 + target] = 1.0
    return table


def on_device(width, count, vector, inverses, lift_maps, jacobians, orient):
    layers, cells = vector.shape[:2]
    elements = layers * cells
    rounds = count.bit_length() - 1
    inv = inverses.reshape(elements, VARS, EXTENT, FACE, BLOCK)
    flat = jacobians.transpose(0, 1, 3, 4, 2, 5).reshape(elements, VARS, VARS, 4, FACE)
    pick = jnp.asarray(picker(), BF16)
    total_nodes = 2 * layers - 1
    depth = 4 * TRACE + -(-elements // 16) * 16
    vmem = pl.BlockSpec(memory_space=pltpu.VMEM)
    result = pl.pallas_call(
        functools.partial(kernel, layers, cells, count, width, rounds),
        out_shape=jax.ShapeDtypeStruct((layers, cells, BLOCK), F32),
        in_specs=[
            pl.BlockSpec(memory_space=pltpu.HBM), vmem, vmem, vmem,
            pl.BlockSpec(memory_space=pltpu.SMEM), vmem,
        ],
        out_specs=vmem,
        scratch_shapes=[
            pltpu.VMEM((elements, EXTENT, VARS, FACE, BLOCK), F32),
            pltpu.SemaphoreType.DMA((elements, EXTENT)),
            pltpu.VMEM((depth, BLOCK), F32),
            pltpu.VMEM((elements, VARS, 8, 128), F32),
            pltpu.VMEM((elements, BLOCK), F32),
            pltpu.VMEM((depth, BLOCK), BF16),
            pltpu.VMEM((depth, BLOCK), BF16),
            pltpu.VMEM((elements, 2 * TRACE, BLOCK), F32),
            pltpu.VMEM((elements, 2 * TRACE, BLOCK), F32),
            pltpu.VMEM((elements, 2 * TRACE, BLOCK), F32),
            pltpu.VMEM((elements, BLOCK), F32),
            pltpu.VMEM((elements, BLOCK), F32),
            pltpu.VMEM((total_nodes * cells, ROWS, WIDE), F32),
            pltpu.VMEM((total_nodes, 8, WIDE), F32),
            pltpu.VMEM((rounds, cells, ROWS, WIDE), F32),
            pltpu.VMEM((rounds, cells, ROWS, WIDE), F32),
            pltpu.SemaphoreType.DMA((rounds, cells)),
            pltpu.SemaphoreType.DMA((rounds, cells)),
            pltpu.SemaphoreType.DMA((2, cells)),
            pltpu.VMEM((rounds, 8, WIDE), F32),
            pltpu.VMEM((rounds, 8, WIDE), F32),
            pltpu.SemaphoreType.DMA((rounds,)),
            pltpu.SemaphoreType.DMA((rounds,)),
            pltpu.VMEM((elements, 128), F32),
            pltpu.VMEM((elements, 128), F32),
            pltpu.VMEM((elements, 128), F32),
            pltpu.VMEM((elements, 128), F32),
            pltpu.VMEM((elements, 128), F32),
            pltpu.VMEM((elements, 128), F32),
            pltpu.SemaphoreType.DMA((4,)),
        ],
        compiler_params=pltpu.CompilerParams(
            collective_id=0, has_side_effects=True, vmem_limit_bytes=62 * 1024 * 1024
        ),
    )(inv, vector, lift_maps.transpose(0, 2, 1), flat, orient.T, pick)
    return result


def solution(mesh):
    in_specs = (
        P("stream", "cross", None),
        P("stream", "cross", None, None),
        P(),
        P("stream", "cross", None, None, None, None),
        P("stream", "cross"),
    )
    out_specs = P("stream", "cross", None)
    return jax.shard_map(
        functools.partial(on_device, mesh.shape["cross"], mesh.shape["stream"]),
        mesh=mesh, in_specs=in_specs, out_specs=out_specs, check_vma=False,
    )
```

```python
import functools

import jax
import jax.numpy as jnp
import numpy as np
from jax import lax
from jax.experimental import pallas as pl
from jax.experimental.pallas import tpu as pltpu
from jax.sharding import PartitionSpec as P

ORDER = 3
EXTENT = ORDER + 1
VARS = 5
FACE = EXTENT * EXTENT
TRACE = VARS * FACE
BLOCK = VARS * FACE * EXTENT
SLOTS = (0, EXTENT - 1) + tuple(range(1, EXTENT - 1))
WIDE = 256
ROWS = TRACE + 8
F32 = jnp.float32
BF16 = jnp.bfloat16


def split(value):
    high = value.astype(BF16)
    return high, (value - high.astype(F32)).astype(BF16)


def product(left, right, transposed=False):
    dims = (((1,), (1 if transposed else 0,)), ((), ()))
    dot = functools.partial(lax.dot_general, dimension_numbers=dims, preferred_element_type=F32)
    left_high, left_low = left
    right_high, right_low = right
    return dot(left_high, right_high) + (dot(left_high, right_low) + dot(left_low, right_high))


def lanes(shape):
    return lax.broadcasted_iota(jnp.int32, shape, 1)


def rows(shape):
    return lax.broadcasted_iota(jnp.int32, shape, 0)


def keep(mask, value):
    return jnp.where(mask, value, 0.0)


def join(left, right):
    lane = lanes((TRACE, WIDE))
    through = jnp.concatenate(
        [jnp.zeros((TRACE, WIDE), F32), keep(lane < 2 * TRACE, right[:TRACE])], axis=0
    )
    first = product(split(left[:, : 2 * TRACE]), split(through))
    lane_all = lanes((ROWS, WIDE))
    row_all = rows((ROWS, WIDE))
    first = first + keep((lane_all >= 2 * TRACE) | (row_all >= TRACE), right)
    back = left[:TRACE]
    moved = pltpu.roll(back, WIDE - 2 * TRACE, 1)
    through = jnp.concatenate(
        [
            keep(lane < TRACE, moved),
            jnp.zeros((TRACE, WIDE), F32),
            keep(lane >= 2 * TRACE, back),
        ],
        axis=0,
    )
    second = product(split(first[:, : 3 * TRACE]), split(through))
    middle = (lane_all >= TRACE) & (lane_all < 2 * TRACE)
    return second + keep(middle, first) + keep(lane_all < TRACE, left)


def apply(column, matrix):
    return jnp.sum(column * matrix, axis=0, keepdims=True)


def stack(parts):
    total = jnp.zeros((8, parts[0].shape[1]), F32)
    row = rows(total.shape)
    for index, part in enumerate(parts):
        total = jnp.where(row == index, jnp.broadcast_to(part, total.shape), total)
    return total


def to_low(value):
    return keep(lanes(value.shape) < TRACE, pltpu.roll(value, WIDE - 2 * TRACE, 1))


def rise(z_left, z_right, left, right):
    lane = lanes((8, WIDE))
    column = z_left.T
    first = z_right + keep(
        lane < 2 * TRACE,
        stack([apply(column[TRACE : 2 * TRACE, c : c + 1], m) for c, m in enumerate(right)]),
    )
    column = first.T
    second = stack([apply(column[:TRACE, c : c + 1], m) for c, m in enumerate(left)])
    return to_low(second) + keep(lane < TRACE, z_left) + keep(lane >= TRACE, first)


def descend(z_in, z_left, z_right, left, right):
    lane = lanes((8, WIDE))
    high = (lane >= TRACE) & (lane < 2 * TRACE)
    column = z_in.T
    inner = keep(
        high,
        z_left + stack([apply(column[TRACE : 2 * TRACE, c : c + 1], m) for c, m in enumerate(left)]),
    )
    passed = stack([apply(column[:TRACE, c : c + 1], m) for c, m in enumerate(right)])
    column = inner.T
    turned = stack([apply(column[TRACE : 2 * TRACE, c : c + 1], m) for c, m in enumerate(right)])
    low = keep(lane < TRACE, z_right + turned) + to_low(passed)
    return low + keep(high, z_in), keep(lane < TRACE, z_in) + inner


def kernel(
    layers, cells, count, width, rounds,
    inv, vector, lift_maps, jacobians, orient, pick, out,
    blocks, block_sem, lhs, jac_rows, natural, lhs_high, lhs_low, lifted, ends, sides, y, x,
    nodes, z_nodes, mine, theirs, send_sem, recv_sem, tail_sems,
    z_mine, z_theirs, z_send, z_recv,
    turns, traces, backs, got_high, got_back, from_left, from_right, cross_sems,
):
    elements = layers * cells
    place = lax.axis_index("stream")
    column_at = lax.axis_index("cross")
    local = layers.bit_length() - 1

    copies = []
    for e in range(elements):
        for slot, i in enumerate(SLOTS):
            copy = pltpu.make_async_copy(inv.at[e, :, i], blocks.at[e, slot], block_sem.at[e, slot])
            copy.start()

    bits = [lax.rem(place // (1 << k), 2) for k in range(rounds)]
    partners = [place + (1 - 2 * bits[k]) * (1 << k) for k in range(rounds)]
    barrier = pltpu.get_barrier_semaphore()
    for k in range(rounds):
        pl.semaphore_signal(barrier, inc=1, device_id=(partners[k], column_at), device_id_type=pl.DeviceIdType.MESH)

    @pl.when(column_at > 0)
    def _():
        pl.semaphore_signal(barrier, inc=1, device_id=(place, column_at - 1), device_id_type=pl.DeviceIdType.MESH)

    @pl.when(column_at < width - 1)
    def _():
        pl.semaphore_signal(barrier, inc=1, device_id=(place, column_at + 1), device_id_type=pl.DeviceIdType.MESH)

    for m in range(4):
        lhs[m * TRACE : (m + 1) * TRACE, :] = lift_maps[m]
    lhs[4 * TRACE :, :] = jnp.zeros((lhs.shape[0] - 4 * TRACE, BLOCK), F32)
    for e in range(elements):
        lhs[4 * TRACE + e : 4 * TRACE + e + 1, :] = vector[e // cells, e % cells : e % cells + 1, :]
        for v in range(VARS):
            for w in range(VARS):
                jac_rows[e, w, :4, v * FACE : (v + 1) * FACE] = jacobians[e, v, w]
    high, low = split(lhs[...])
    lhs_high[...] = high
    lhs_low[...] = low
    z_nodes[...] = jnp.zeros_like(z_nodes)
    z_mine[...] = jnp.zeros_like(z_mine)
    backs[...] = jnp.zeros_like(backs)

    lane = lanes((TRACE, WIDE))

    row_face = rows((TRACE, TRACE))
    lane_face = lanes((TRACE, TRACE))
    same = lax.rem(row_face, FACE) == lax.rem(lane_face, FACE)

    def source_of(code, node_index):
        first = lax.div(node_index, EXTENT)
        second = node_index - first * EXTENT
        first, second = (
            first + lax.rem(code, 2) * (second - first),
            second + lax.rem(code, 2) * (first - second),
        )
        first = first + lax.rem(code // 2, 2) * (EXTENT - 1 - 2 * first)
        second = second + lax.rem(code // 4, 2) * (EXTENT - 1 - 2 * second)
        return first * EXTENT + second

    def face(e, m, chosen):
        tall = jnp.concatenate(
            [jnp.broadcast_to(jac_rows[e, w, m : m + 1, :TRACE], (FACE, TRACE)) for w in range(VARS)],
            axis=0,
        )
        return keep(chosen, tall)

    def prepare_layer(layer, carry):
        for c in range(cells):
            prepare(layer * cells + c)
        return carry

    def prepare(e):
        for slot, i in enumerate(SLOTS):
            pltpu.make_async_copy(inv.at[e, :, i], blocks.at[e, slot], block_sem.at[e, slot]).wait()
        block = split(blocks[e].reshape(BLOCK, BLOCK))
        through = product((lhs_high[...], lhs_low[...]), block, transposed=True)
        row_values = through[4 * TRACE : 4 * TRACE + elements]
        own = jnp.sum(keep(rows(row_values.shape) == e, row_values), axis=0, keepdims=True)
        y[pl.ds(e, 1), :] = own
        lifted[e] = through[2 * TRACE : 4 * TRACE]
        upward = -product(split(face(e, 0, same)), split(through[:TRACE]))
        downward = -product(split(face(e, 1, same)), split(through[TRACE : 2 * TRACE]))
        ends[e, :TRACE] = downward
        ends[e, TRACE:] = upward
        matrix = keep(lane < 2 * TRACE, upward[:, :WIDE]) + pltpu.roll(
            keep(lane < TRACE, downward[:, :WIDE]), 2 * TRACE, 1
        )
        nodes[e, :TRACE] = matrix
        bottom = keep(lanes((8, WIDE)) < 2 * TRACE, jnp.broadcast_to(own[:, :WIDE], (8, WIDE)))
        nodes[e, TRACE:] = keep(rows((8, WIDE)) == 0, bottom)

    lax.fori_loop(0, layers, prepare_layer, 0)

    sides_met = jnp.minimum(column_at, 1) + jnp.minimum(width - 1 - column_at, 1)
    pl.semaphore_wait(barrier, rounds + sides_met)

    starts = []
    base = 0
    for level in range(local + 1):
        starts.append(base)
        base += layers >> level

    def node(level, index, c):
        return (starts[level] + index) * cells + c

    def remote(source, target, send, recv, device):
        return pltpu.make_async_remote_copy(
            src_ref=source, dst_ref=target, send_sem=send, recv_sem=recv,
            device_id=device, device_id_type=pl.DeviceIdType.MESH,
        )

    sent = []
    pending = {}

    def dispatch(k, c):
        device = (partners[k], column_at)
        send, recv = send_sem.at[k, c], recv_sem.at[k, c]
        if k < rounds - 1:
            pending[k, c] = [remote(mine.at[k, c], theirs.at[k, c], send, recv, device)]
        else:
            first, second = pl.ds(0, 128), pl.ds(128, 128)
            bottom = pl.ds(TRACE, 8)
            pending[k, c] = [
                remote(mine.at[k, c, :, first], theirs.at[k, c, :, first], send, recv, device),
                remote(
                    mine.at[k, c, bottom, second], theirs.at[k, c, bottom, second],
                    tail_sems.at[0, c], tail_sems.at[1, c], device,
                ),
            ]
        for copy in pending[k, c]:
            copy.start()
            sent.append(copy)

    for c in range(cells):
        for level in range(local):
            for index in range(layers >> (level + 1)):
                nodes[node(level + 1, index, c)] = join(
                    nodes[node(level, 2 * index, c)], nodes[node(level, 2 * index + 1, c)]
                )
        mine[0, c] = nodes[node(local, 0, c)]
        dispatch(0, c)

    def prepare_sides(layer, carry):
        for c in range(cells):
            e = layer * cells + c
            chosen = lax.rem(row_face, FACE) == source_of(orient[c, layer], lax.rem(lane_face, FACE))
            sides[e, :TRACE] = product(split(face(e, 2, chosen)), split(lifted[e, :TRACE]))
            sides[e, TRACE:] = product(split(face(e, 3, same)), split(lifted[e, TRACE:]))
        return carry

    def prepare_turns(layer, carry):
        within = row_face - block_row * FACE
        for c in range(cells):
            turn = (block_row == block_lane) & (source_of(orient[c, layer], within) == face_lane)
            turns[layer * cells + c] = turn.astype(F32)
        return carry

    block_row, block_lane = lax.div(row_face, FACE), lax.div(lane_face, FACE)
    face_lane = lane_face - block_lane * FACE

    for k in range(rounds):
        if k == 0:
            lax.fori_loop(0, layers, prepare_sides, 0)
        if k == 1 % rounds:
            lax.fori_loop(0, layers, prepare_turns, 0)
        for c in range(cells):
            for copy in pending[k, c]:
                copy.wait_recv()
            if k < rounds - 1:
                flag = bits[k] == 1
                ours, other = mine[k, c], theirs[k, c]
                mine[k + 1, c] = join(jnp.where(flag, other, ours), jnp.where(flag, ours, other))
                dispatch(k + 1, c)

    def ordered(k, c):
        flag = bits[k] == 1
        ours, other = mine[k, c, :TRACE], theirs[k, c, :TRACE]
        return jnp.where(flag, other, ours), jnp.where(flag, ours, other)

    def fall(z_pairs):
        lane_z = lanes((8, WIDE))
        z_in = None
        for k in reversed(range(rounds)):
            flag = bits[k] == 1
            ours, other = z_pairs[k]
            z_left, z_right = jnp.where(flag, other, ours), jnp.where(flag, ours, other)
            if z_in is None:
                column = z_left.T
                turned = stack([
                    apply(column[TRACE : 2 * TRACE, c : c + 1], theirs[k, c, :TRACE, :128])
                    for c in range(cells)
                ])
                turned = jnp.concatenate([turned, jnp.zeros((8, WIDE - 128), F32)], axis=1)
                z_low = keep(lane_z < TRACE, z_right + turned)
                z_high = keep((lane_z >= TRACE) & (lane_z < 2 * TRACE), z_left)
            else:
                pairs = [ordered(k, c) for c in range(cells)]
                z_low, z_high = descend(
                    z_in, z_left, z_right, [p[0] for p in pairs], [p[1] for p in pairs]
                )
            z_in = jnp.where(flag, z_high, z_low)
        entering = [z_in]
        for level in reversed(range(local)):
            following = []
            for index in range(layers >> (level + 1)):
                left = [nodes[node(level, 2 * index, c), :TRACE] for c in range(cells)]
                right = [nodes[node(level, 2 * index + 1, c), :TRACE] for c in range(cells)]
                following += list(
                    descend(
                        entering[index],
                        z_nodes[starts[level] + 2 * index],
                        z_nodes[starts[level] + 2 * index + 1],
                        left,
                        right,
                    )
                )
            entering = following
        for layer in range(layers):
            column = entering[layer].T
            for c in range(cells):
                e = layer * cells + c
                x[e : e + 1, :] = y[e : e + 1, :] + apply(column[: 2 * TRACE, c : c + 1], ends[e])

    for level in range(local):
        for index in range(layers >> level):
            for c in range(cells):
                z_nodes[starts[level] + index, c : c + 1, :] = nodes[node(level, index, c), TRACE : TRACE + 1]
    fall([
        (
            stack([mine[k, c, TRACE : TRACE + 1] for c in range(cells)]),
            stack([theirs[k, c, TRACE : TRACE + 1] for c in range(cells)]),
        )
        for k in range(rounds)
    ])

    x_high, x_low = split(x[...])
    cross = jnp.dot(x_high, pick[...], preferred_element_type=F32) + jnp.dot(
        x_low, pick[...], preferred_element_type=F32
    )
    traces[...] = cross[:, 128:]
    column = cross[:, :128].T
    for e in range(elements):
        backs[e : e + 1, :TRACE] = apply(column[:TRACE, e : e + 1], turns[e])
    up = remote(traces, got_high, cross_sems.at[0], cross_sems.at[1], (place, lax.rem(column_at + 1, width)))
    down = remote(backs, got_back, cross_sems.at[2], cross_sems.at[3], (place, lax.rem(column_at + width - 1, width)))

    @pl.when(column_at < width - 1)
    def _():
        up.start()

    @pl.when(column_at > 0)
    def _():
        down.start()

    for layer in range(layers):
        for c in range(cells):
            e = layer * cells + c
            if c > 0:
                from_left[e : e + 1, :] = traces[e - 1 : e, :]
            if c < cells - 1:
                from_right[e : e + 1, :] = backs[e + 1 : e + 2, :]
    firsts = [layer * cells for layer in range(layers)]
    lasts = [layer * cells + cells - 1 for layer in range(layers)]

    @pl.when(column_at > 0)
    def _():
        up.wait_recv()
        for first, last in zip(firsts, lasts):
            from_left[first : first + 1, :] = got_high[last : last + 1, :]

    @pl.when(column_at == 0)
    def _():
        for first in firsts:
            from_left[first : first + 1, :] = jnp.zeros((1, 128), F32)

    @pl.when(column_at < width - 1)
    def _():
        down.wait_recv()
        for first, last in zip(firsts, lasts):
            from_right[last : last + 1, :] = got_back[first : first + 1, :]

    @pl.when(column_at == width - 1)
    def _():
        for last in lasts:
            from_right[last : last + 1, :] = jnp.zeros((1, 128), F32)

    left_columns = from_left[...].T
    right_columns = from_right[...].T
    lane_row = lanes((1, WIDE))
    for layer in range(layers):
        for c in range(cells):
            e = layer * cells + c
            value = y[e : e + 1, :] - (
                apply(left_columns[:TRACE, e : e + 1], sides[e, :TRACE])
                + apply(right_columns[:TRACE, e : e + 1], sides[e, TRACE:])
            )
            y[e : e + 1, :] = value
            z_nodes[starts[0] + layer, c : c + 1, :] = keep(lane_row < 2 * TRACE, value[:, :WIDE])

    for level in range(local):
        for index in range(layers >> (level + 1)):
            left = [nodes[node(level, 2 * index, c), :TRACE] for c in range(cells)]
            right = [nodes[node(level, 2 * index + 1, c), :TRACE] for c in range(cells)]
            z_nodes[starts[level + 1] + index] = rise(
                z_nodes[starts[level] + 2 * index], z_nodes[starts[level] + 2 * index + 1], left, right
            )
    z_mine[0] = z_nodes[starts[local]]
    for k in range(rounds):
        copy = remote(z_mine.at[k], z_theirs.at[k], z_send.at[k], z_recv.at[k], (partners[k], column_at))
        copy.start()
        sent.append(copy)
        if k < rounds - 1:
            pairs = [ordered(k, c) for c in range(cells)]
        copy.wait_recv()
        if k < rounds - 1:
            flag = bits[k] == 1
            ours, other = z_mine[k], z_theirs[k]
            z_mine[k + 1] = rise(
                jnp.where(flag, other, ours), jnp.where(flag, ours, other),
                [p[0] for p in pairs], [p[1] for p in pairs],
            )
    fall([(z_mine[k], z_theirs[k]) for k in range(rounds)])
    for slot, i in enumerate(SLOTS):
        for v in range(VARS):
            target = (v * EXTENT + i) * FACE
            source = slot * TRACE + v * FACE
            natural[:, target : target + FACE] = x[:, source : source + FACE]
    for layer in range(layers):
        out[layer] = natural[layer * cells : (layer + 1) * cells, :]

    for copy in sent:
        copy.wait_send()

    @pl.when(column_at < width - 1)
    def _():
        up.wait_send()

    @pl.when(column_at > 0)
    def _():
        down.wait_send()


def picker():
    table = np.zeros((BLOCK, WIDE), np.float32)
    for slot, i in enumerate(SLOTS):
        for v in range(VARS):
            for k in range(EXTENT):
                source = slot * TRACE + v * FACE + k
                target = v * FACE + i * EXTENT + k
                table[source, target] = 1.0
                table[source + (EXTENT - 1) * EXTENT, 128 + target] = 1.0
    return table


def on_device(width, count, vector, inverses, lift_maps, jacobians, orient):
    layers, cells = vector.shape[:2]
    elements = layers * cells
    rounds = count.bit_length() - 1
    inv = inverses.reshape(elements, VARS, EXTENT, FACE, BLOCK)
    flat = jacobians.transpose(0, 1, 3, 4, 2, 5).reshape(elements, VARS, VARS, 4, FACE)
    pick = jnp.asarray(picker(), BF16)
    total_nodes = 2 * layers - 1
    depth = 4 * TRACE + -(-elements // 16) * 16
    vmem = pl.BlockSpec(memory_space=pltpu.VMEM)
    result = pl.pallas_call(
        functools.partial(kernel, layers, cells, count, width, rounds),
        out_shape=jax.ShapeDtypeStruct((layers, cells, BLOCK), F32),
        in_specs=[
            pl.BlockSpec(memory_space=pltpu.HBM), vmem, vmem, vmem,
            pl.BlockSpec(memory_space=pltpu.SMEM), vmem,
        ],
        out_specs=vmem,
        scratch_shapes=[
            pltpu.VMEM((elements, EXTENT, VARS, FACE, BLOCK), F32),
            pltpu.SemaphoreType.DMA((elements, EXTENT)),
            pltpu.VMEM((depth, BLOCK), F32),
            pltpu.VMEM((elements, VARS, 8, 128), F32),
            pltpu.VMEM((elements, BLOCK), F32),
            pltpu.VMEM((depth, BLOCK), BF16),
            pltpu.VMEM((depth, BLOCK), BF16),
            pltpu.VMEM((elements, 2 * TRACE, BLOCK), F32),
            pltpu.VMEM((elements, 2 * TRACE, BLOCK), F32),
            pltpu.VMEM((elements, 2 * TRACE, BLOCK), F32),
            pltpu.VMEM((elements, BLOCK), F32),
            pltpu.VMEM((elements, BLOCK), F32),
            pltpu.VMEM((total_nodes * cells, ROWS, WIDE), F32),
            pltpu.VMEM((total_nodes, 8, WIDE), F32),
            pltpu.VMEM((rounds, cells, ROWS, WIDE), F32),
            pltpu.VMEM((rounds, cells, ROWS, WIDE), F32),
            pltpu.SemaphoreType.DMA((rounds, cells)),
            pltpu.SemaphoreType.DMA((rounds, cells)),
            pltpu.SemaphoreType.DMA((2, cells)),
            pltpu.VMEM((rounds, 8, WIDE), F32),
            pltpu.VMEM((rounds, 8, WIDE), F32),
            pltpu.SemaphoreType.DMA((rounds,)),
            pltpu.SemaphoreType.DMA((rounds,)),
            pltpu.VMEM((elements, TRACE, TRACE), F32),
            pltpu.VMEM((elements, 128), F32),
            pltpu.VMEM((elements, 128), F32),
            pltpu.VMEM((elements, 128), F32),
            pltpu.VMEM((elements, 128), F32),
            pltpu.VMEM((elements, 128), F32),
            pltpu.VMEM((elements, 128), F32),
            pltpu.SemaphoreType.DMA((4,)),
        ],
        compiler_params=pltpu.CompilerParams(
            collective_id=0, has_side_effects=True, vmem_limit_bytes=62 * 1024 * 1024
        ),
    )(inv, vector, lift_maps.transpose(0, 2, 1), flat, orient.T, pick)
    return result


def solution(mesh):
    in_specs = (
        P("stream", "cross", None),
        P("stream", "cross", None, None),
        P(),
        P("stream", "cross", None, None, None, None),
        P("stream", "cross"),
    )
    out_specs = P("stream", "cross", None)
    return jax.shard_map(
        functools.partial(on_device, mesh.shape["cross"], mesh.shape["stream"]),
        mesh=mesh, in_specs=in_specs, out_specs=out_specs, check_vma=False,
    )
```
